32 devices in a mesh: dp: 2 (over core), row: 4 (over y, x), col: 4 (over z).
Axes of the slice: x: 2, y: 2, z: 4, core: 2. Of those that a mesh axis runs over, the one named last changes fastest.
Arguments:
- tokens: bfloat16 [1024, 768], P(('dp', 'col'), 'row'), may hold values from -150 to 150
- out_grad: bfloat16 [1024, 768], P(('dp', 'col'), 'row'), may hold values from -6 to 6
- segment_ids: int32 [2, 512], P('dp'), may hold values from 0 to 1, never falling along the last dimension, each value on 1 to 384 neighbouring positions
- w_qkv: bfloat16 [768, 2304], P('row', 'col'), may hold values from -8 to 8
- w_out: bfloat16 [768, 768], P('col', 'row'), may hold values from -0.875 to 0.875
- w_fc: bfloat16 [768, 3072], P('row', 'col'), may hold values from -0.21875 to 0.21875
- w_proj: bfloat16 [3072, 768], P('col', 'row'), may hold values from -0.109375 to 0.109375
- bias_qkv: float32 [2304], P('col'), may hold values from -1.8 to 1.8
- bias_fc: float32 [3072], P('col'), may hold values from -1.8 to 1.8
- row_vectors: float32 [6, 768], P(None, 'row'), may hold values from -0.6 to 1.5
- mom_qkv: float32 [768, 2304], P('row', 'col'), may hold values from -20 to 20
- mom_out: float32 [768, 768], P('col', 'row'), may hold values from -20 to 20
- mom_fc: float32 [768, 3072], P('row', 'col'), may hold values from -20 to 20
- mom_proj: float32 [3072, 768], P('col', 'row'), may hold values from -20 to 20
- mom_bias_qkv: float32 [2304], P('col'), may hold values from -20 to 20
- mom_bias_fc: float32 [3072], P('col'), may hold values from -20 to 20
- mom_rows: float32 [6, 768], P(None, 'row'), may hold values from -20 to 20
Outputs:
- block_out: bfloat16 [1024, 768], P(('dp', 'col'), 'row')
- input_grad: float32 [1024, 768], P(('dp', 'col'), 'row')
- grad_qkv: float32 [768, 2304], P('row', 'col')
- grad_out: float32 [768, 768], P('col', 'row')
- grad_fc: float32 [768, 3072], P('row', 'col')
- grad_proj: float32 [3072, 768], P('col', 'row')
- grad_bias_qkv: float32 [2304], P('col')
- grad_bias_fc: float32 [3072], P('col')
- grad_rows: float32 [6, 768], P(None, 'row')
- new_qkv: float32 [768, 2304], P('row', 'col')
- new_out: float32 [768, 768], P('col', 'row')
- new_fc: float32 [768, 3072], P('row', 'col')
- new_proj: float32 [3072, 768], P('col', 'row')
- new_bias_qkv: float32 [2304], P('col')
- new_bias_fc: float32 [3072], P('col')
- new_rows: float32 [6, 768], P(None, 'row')
- new_mom_qkv: float32 [768, 2304], P('row', 'col')
- new_mom_out: float32 [768, 768], P('col', 'row')
- new_mom_fc: float32 [768, 3072], P('row', 'col')
- new_mom_proj: float32 [3072, 768], P('col', 'row')
- new_mom_bias_qkv: float32 [2304], P('col')
- new_mom_bias_fc: float32 [3072], P('col')
- new_mom_rows: float32 [6, 768], P(None, 'row')
The draws below stay inside these ranges and needn't reach their ends.
Inputs may be any that keep to these rules, and one draw needn't show every extreme that they name: `segment_ids`: within each data group the segment numbers never fall; the group's 2 sequences have 512 tokens together, each at most 384.
All inputs are finite; a program needn't handle non-finite values.
Results may differ from the reference program's by a relative error of at most 0.012.
Values may be sent and summed in bfloat16 or wider, within the bound.
A program may use at most 128 MiB of HBM per device.

```python
import math
import jax
import jax.numpy as jnp
import numpy as np
from jax import lax

D = 768
HEADS = 12
HD = 64
FF = 3072
TOK_G = 512
NS_STEPS = 2
SEGS = 2
GROUPS = 2
TOKENS = 1024
LONGEST = 384


def draw_tokens(key, part):
    sub_keys = jax.random.split(key, 3)
    rising = 3.0 ** (jnp.arange(D, dtype=jnp.float32) / D)
    spread = jnp.exp(jax.random.uniform(sub_keys[1], (D,), jnp.float32, 0.0, math.log(10.0)))
    column = rising * spread / 5.0
    offset = jnp.clip(jax.random.normal(sub_keys[2], (D,), jnp.float32), -2.0, 2.0) * 0.5
    base = jnp.clip(jax.random.normal(sub_keys[0], (TOKENS, D), jnp.float32), -4.0, 4.0)
    return ((base + offset) * column).astype(jnp.bfloat16)


def draw_w_qkv(key, part):
    sub_keys = jax.random.split(key, 1)
    base = jnp.clip(jax.random.normal(sub_keys[0], (D, HEADS, 3, HD), jnp.float32), -4.0, 4.0) / math.sqrt(D)
    return base.reshape(D, 3 * D).astype(jnp.bfloat16)


def draw_row_vectors(key, part):
    sub_keys = jax.random.split(key, 2)
    gains = jax.random.uniform(sub_keys[0], (6, D), jnp.float32, 0.5, 1.5)
    shifts = jnp.clip(jax.random.normal(sub_keys[1], (6, D), jnp.float32), -3.0, 3.0) * 0.2
    which_rows = jnp.arange(6, dtype=jnp.int32)
    picked = (which_rows % 2 == 0) & (which_rows < 4)
    return jnp.where(picked[:, None], gains, shifts)


def block_scale(own_key, shape, cuts, least, largest):
    level, own = 1.0, jax.random.fold_in(own_key, 6)
    for position, blocks in cuts:
        steps = jnp.exp(jax.random.uniform(jax.random.fold_in(own, position), (blocks,), jnp.float32, least / len(cuts), largest / len(cuts)))
        level = level * jnp.repeat(steps, shape[position] // blocks).reshape([-1 if axis == position else 1 for axis in range(len(shape))])
    return level


def length_profile(count, total, most, skew):
    portions = [(1 << 20) // math.isqrt(rank ** skew) + 1 for rank in range(2, count + 1)]
    rest, counts = total - most - (count - 1), [1] * (count - 1)
    while rest > 0:
        free = [i for i in range(count - 1) if counts[i] < most]
        mass, remaining = sum([portions[i] for i in free]), rest
        for i in free:
            extra = min(most - counts[i], max(1, remaining * portions[i] // mass), rest)
            counts[i] = counts[i] + extra
            rest = rest - extra
    return np.array([most] + counts)


def uneven_parts(own_key, number_of, total, limit, lean):
    if number_of == 2:
        one = jax.random.randint(own_key, (), max(1, total - limit), min(limit, total - 1) + 1)
        return jnp.stack([one, total - one])
    sizes = jnp.asarray(length_profile(number_of, total, limit, lean), jnp.int32)
    couples = (number_of - 1) // 2
    source_of, taker = sizes[1:1 + 2 * couples:2], sizes[2:2 + 2 * couples:2]
    slack = jnp.minimum(source_of - 1, limit - taker)
    passed = jax.random.randint(jax.random.fold_in(own_key, 1), (couples,), 0, 1 << 20) % (slack + 1)
    sizes = sizes.at[1:1 + 2 * couples:2].set(source_of - passed).at[2:2 + 2 * couples:2].set(taker + passed)
    return sizes[jax.random.permutation(jax.random.fold_in(own_key, 2), number_of)]


def noise(stream_key, dims, scale, bound, shards=(), kind=jnp.bfloat16):
    gain = block_scale(stream_key, dims, shards, -0.22, 0.18) if shards else 1.0
    result = jax.random.normal(stream_key, dims, jnp.float32) * scale * gain
    return jnp.minimum(jnp.maximum(result, -bound), bound).astype(kind)


def setup_inputs(seed: int = 0) -> dict:
    splits = jax.random.split(jax.random.key(seed), 18)
    return {
        "tokens": draw_tokens(jax.random.fold_in(splits[17], 71), 0),
        "out_grad": noise(splits[1], (TOKENS, D), 1.0, 6.0, ((0, 8), (1, 4))),
        "segment_ids": jax.vmap(lambda own: jnp.searchsorted(jnp.cumsum(uneven_parts(own, SEGS, TOK_G, LONGEST, 2)), jnp.arange(TOK_G), side="right"))(jax.random.split(splits[2], GROUPS)).reshape((GROUPS, TOK_G)).astype(jnp.int32),
        "w_qkv": draw_w_qkv(jax.random.fold_in(splits[17], 71), 0),
        "w_out": noise(splits[4], (D, D), (D // 16) ** -0.5, 0.875, ((0, 4), (1, 4))),
        "w_fc": noise(splits[5], (D, FF), D ** -0.5, 0.21875, ((0, 4), (1, 4))),
        "w_proj": noise(splits[6], (FF, D), FF ** -0.5, 0.109375, ((0, 4), (1, 4))),
        "bias_qkv": noise(splits[7], (3 * D,), 0.3, 1.8, ((0, 4),), jnp.float32),
        "bias_fc": noise(splits[8], (FF,), 0.3, 1.8, ((0, 4),), jnp.float32),
        "row_vectors": draw_row_vectors(jax.random.fold_in(splits[17], 71), 0),
        "mom_qkv": noise(splits[10], (D, 3 * D), (0.1 * TOKENS ** 0.5), 20.0, ((0, 4), (1, 4)), jnp.float32),
        "mom_out": noise(splits[11], (D, D), (0.1 * TOKENS ** 0.5), 20.0, ((0, 4), (1, 4)), jnp.float32),
        "mom_fc": noise(splits[12], (D, FF), (0.1 * TOKENS ** 0.5), 20.0, ((0, 4), (1, 4)), jnp.float32),
        "mom_proj": noise(splits[13], (FF, D), (0.1 * TOKENS ** 0.5), 20.0, ((0, 4), (1, 4)), jnp.float32),
        "mom_bias_qkv": noise(splits[14], (3 * D,), (0.1 * TOKENS ** 0.5), 20.0, ((0, 4),), jnp.float32),
        "mom_bias_fc": noise(splits[15], (FF,), (0.1 * TOKENS ** 0.5), 20.0, ((0, 4),), jnp.float32),
        "mom_rows": noise(splits[16], (6, D), (0.1 * TOKENS ** 0.5), 20.0, ((1, 4),), jnp.float32),
    }


eps_norm = 1e-05
eps_gram = 1e-06
coef_a = 3.4445
coef_b = -4.775
coef_c = 2.0315
beta_mom = 0.95
rate_matrix = 0.03
rate_vector = 0.6

def round_low(values):
    return lax.optimization_barrier(values.astype(jnp.bfloat16)).astype(jnp.float32)

def gelu_value(values):
    return jax.nn.gelu(values, approximate=True)

def gelu_slope(values):
    return jax.vjp(gelu_value, values)[1](jnp.ones_like(values))[0]

def norm_forward(values, gain_row, shift_row):
    mean_row = lax.optimization_barrier(jnp.mean(values, axis=1, keepdims=True))
    square = lax.optimization_barrier(jnp.mean(values * values, axis=1, keepdims=True))
    inv_std = lax.rsqrt(square - mean_row * mean_row + eps_norm)
    unit_rows = (values - mean_row) * inv_std
    return (unit_rows, inv_std, unit_rows * gain_row + shift_row)

def norm_backward(grad_rows, unit_rows, inv_std, gain_row):
    scaled = grad_rows * gain_row
    first_mean = lax.optimization_barrier(jnp.mean(scaled, axis=1, keepdims=True))
    second_mean = lax.optimization_barrier(jnp.mean(scaled * unit_rows, axis=1, keepdims=True))
    return inv_std * (scaled - first_mean - unit_rows * second_mean)

def wide_einsum(form, left_side, right_side):
    return jnp.einsum(form, left_side.astype(jnp.float32), right_side.astype(jnp.float32), precision=lax.Precision.HIGHEST)

def attend_forward(query_rows, key_rows, value_rows, allowed, score_scale):
    scores = wide_einsum('qhe,khe->hqk', query_rows, key_rows) * score_scale
    scores = jnp.where(allowed[None], scores, -jnp.inf)
    row_max = lax.optimization_barrier(jnp.max(scores, axis=2, keepdims=True))
    log_total = row_max + jnp.log(lax.optimization_barrier(jnp.sum(jnp.exp(scores - row_max), axis=2, keepdims=True)))
    prob_low = round_low(jnp.exp(scores - log_total))
    attended = wide_einsum('hqk,khe->qhe', prob_low, value_rows)
    return (attended.astype(jnp.bfloat16), log_total)

def attend_grad(query_rows, key_rows, value_rows, allowed, score_scale, grad_low, attended, log_total):
    scores = wide_einsum('qhe,khe->hqk', query_rows, key_rows) * score_scale
    scores = jnp.where(allowed[None], scores, -jnp.inf)
    probs_full = jnp.exp(scores - log_total)
    prob_low = round_low(probs_full)
    grad_value = wide_einsum('hqk,qhe->khe', prob_low, grad_low)
    grad_probs = wide_einsum('qhe,khe->hqk', grad_low, value_rows)
    row_dot = lax.optimization_barrier(jnp.sum(grad_low.astype(jnp.float32) * attended.astype(jnp.float32), axis=2)).T[:, :, None]
    grad_scores = round_low(score_scale * probs_full * (grad_probs - row_dot))
    grad_query = wide_einsum('hqk,khe->qhe', grad_scores, key_rows)
    grad_key = wide_einsum('hqk,qhe->khe', grad_scores, query_rows)
    return (grad_query, grad_key, grad_value)

def orthogonalize(update_low):
    flipped = update_low.shape[0] > update_low.shape[1]
    matrix = update_low.T if flipped else update_low
    gram_matrix = jnp.dot(matrix, matrix.T, preferred_element_type=jnp.float32)
    gram_norm = jnp.sqrt(jnp.sum(gram_matrix * gram_matrix)) + eps_gram
    current = (matrix.astype(jnp.float32) / jnp.sqrt(gram_norm)).astype(jnp.bfloat16)
    gram_low = (gram_matrix / gram_norm).astype(jnp.bfloat16)
    for repeat in range(NS_STEPS):
        if repeat > 0:
            gram_low = jnp.dot(current, current.T, preferred_element_type=jnp.float32).astype(jnp.bfloat16)
        polynomial = (coef_b * gram_low.astype(jnp.float32) + coef_c * jnp.dot(gram_low, gram_low, preferred_element_type=jnp.float32)).astype(jnp.bfloat16)
        current = (coef_a * current.astype(jnp.float32) + jnp.dot(polynomial, current, preferred_element_type=jnp.float32)).astype(jnp.bfloat16)
    return current.T if flipped else current

def reference(tokens, out_grad, segment_ids, w_qkv, w_out, w_fc, w_proj, bias_qkv, bias_fc, row_vectors, mom_qkv, mom_out, mom_fc, mom_proj, mom_bias_qkv, mom_bias_fc, mom_rows):
    score_scale = 1.0 / math.sqrt(HD)
    gain_one = row_vectors[0]
    shift_one = row_vectors[1]
    gain_two = row_vectors[2]
    shift_two = row_vectors[3]
    bias_out = row_vectors[4]
    bias_proj = row_vectors[5]
    positions = jnp.arange(TOK_G, dtype=jnp.int32)

    def group_pass(carry, inputs):
        tok_group, grad_group, seg_group = inputs
        resid_in = tok_group.astype(jnp.float32)
        unit_one, inv_one, normed_one = norm_forward(resid_in, gain_one, shift_one)
        act_one = normed_one.astype(jnp.bfloat16)
        qkv_all = (jnp.dot(act_one, w_qkv, preferred_element_type=jnp.float32) + bias_qkv).astype(jnp.bfloat16)
        qkv_tiles = qkv_all.reshape(TOK_G, HEADS, 3, HD)
        query_rows = qkv_tiles[:, :, 0]
        key_rows = qkv_tiles[:, :, 1]
        value_rows = qkv_tiles[:, :, 2]
        allowed = (positions[None, :] <= positions[:, None]) & (seg_group[None, :] == seg_group[:, None])
        attended, log_total = attend_forward(query_rows, key_rows, value_rows, allowed, score_scale)
        attn_flat = attended.reshape(TOK_G, D)
        resid_mid = resid_in + jnp.dot(attn_flat, w_out, preferred_element_type=jnp.float32) + bias_out
        unit_two, inv_two, normed_two = norm_forward(resid_mid, gain_two, shift_two)
        act_two = normed_two.astype(jnp.bfloat16)
        hidden_pre = jnp.dot(act_two, w_fc, preferred_element_type=jnp.float32) + bias_fc
        hidden = gelu_value(hidden_pre).astype(jnp.bfloat16)
        block_out = (resid_mid + jnp.dot(hidden, w_proj, preferred_element_type=jnp.float32) + bias_proj).astype(jnp.bfloat16)
        grad_hidden = jnp.dot(grad_group, w_proj.T, preferred_element_type=jnp.float32)
        grad_pre = (gelu_slope(hidden_pre) * grad_hidden).astype(jnp.bfloat16)
        grad_w_proj = jnp.dot(hidden.T, grad_group, preferred_element_type=jnp.float32)
        grad_w_fc = jnp.dot(act_two.T, grad_pre, preferred_element_type=jnp.float32)
        grad_b_fc = lax.optimization_barrier(jnp.sum(grad_pre.astype(jnp.float32), axis=0))
        grad_norm_two = jnp.dot(grad_pre, w_fc.T, preferred_element_type=jnp.float32)
        grad_mid = grad_group.astype(jnp.float32) + norm_backward(grad_norm_two, unit_two, inv_two, gain_two)
        grad_mid_low = grad_mid.astype(jnp.bfloat16)
        grad_w_out = jnp.dot(attn_flat.T, grad_mid_low, preferred_element_type=jnp.float32)
        grad_attn = jnp.dot(grad_mid_low, w_out.T, preferred_element_type=jnp.float32).astype(jnp.bfloat16)
        grad_query, grad_key, grad_value = attend_grad(query_rows, key_rows, value_rows, allowed, score_scale, grad_attn.reshape(TOK_G, HEADS, HD), attended, log_total)
        grad_qkv = jnp.stack([grad_query, grad_key, grad_value], axis=2).reshape(TOK_G, 3 * D).astype(jnp.bfloat16)
        grad_w_qkv = jnp.dot(act_one.T, grad_qkv, preferred_element_type=jnp.float32)
        grad_b_qkv = lax.optimization_barrier(jnp.sum(grad_qkv.astype(jnp.float32), axis=0))
        grad_norm_one = jnp.dot(grad_qkv, w_qkv.T, preferred_element_type=jnp.float32)
        input_grad = grad_mid + norm_backward(grad_norm_one, unit_one, inv_one, gain_one)
        row_terms = jnp.stack([lax.optimization_barrier(jnp.sum(grad_norm_one * unit_one, axis=0)), lax.optimization_barrier(jnp.sum(grad_norm_one, axis=0)), lax.optimization_barrier(jnp.sum(grad_norm_two * unit_two, axis=0)), lax.optimization_barrier(jnp.sum(grad_norm_two, axis=0)), lax.optimization_barrier(jnp.sum(grad_mid_low.astype(jnp.float32), axis=0)), lax.optimization_barrier(jnp.sum(grad_group.astype(jnp.float32), axis=0))])
        terms = (grad_w_qkv, grad_w_out, grad_w_fc, grad_w_proj, grad_b_qkv, grad_b_fc, row_terms)
        new_carry = tuple((previous + current for previous, current in zip(carry, terms)))
        return (new_carry, (block_out, input_grad))
    start_carry = (jnp.zeros((D, 3 * D), jnp.float32), jnp.zeros((D, D), jnp.float32), jnp.zeros((D, FF), jnp.float32), jnp.zeros((FF, D), jnp.float32), jnp.zeros((3 * D,), jnp.float32), jnp.zeros((FF,), jnp.float32), jnp.zeros((6, D), jnp.float32))
    sums, outputs = lax.scan(group_pass, start_carry, (tokens.reshape(GROUPS, TOK_G, D), out_grad.reshape(GROUPS, TOK_G, D), segment_ids))
    block_out = outputs[0].reshape(TOKENS, D)
    input_grad = outputs[1].reshape(TOKENS, D)

    def matrix_step(weight, gradient, moment):
        new_moment = beta_mom * moment + gradient
        pushed = (gradient + beta_mom * new_moment).astype(jnp.bfloat16)
        ortho = orthogonalize(pushed)
        factor = rate_matrix * math.sqrt(max(weight.shape[0], weight.shape[1]))
        return (weight.astype(jnp.float32) - factor * ortho.astype(jnp.float32), new_moment)

    def vector_step(weight, gradient, moment):
        new_moment = beta_mom * moment + gradient
        return (weight - rate_vector / math.sqrt(TOKENS) * (gradient + beta_mom * new_moment), new_moment)
    new_qkv, new_mom_qkv = matrix_step(w_qkv, sums[0], mom_qkv)
    new_out, new_mom_out = matrix_step(w_out, sums[1], mom_out)
    new_fc, new_mom_fc = matrix_step(w_fc, sums[2], mom_fc)
    new_proj, new_mom_proj = matrix_step(w_proj, sums[3], mom_proj)
    new_bias_qkv, new_mom_bias_qkv = vector_step(bias_qkv, sums[4], mom_bias_qkv)
    new_bias_fc, new_mom_bias_fc = vector_step(bias_fc, sums[5], mom_bias_fc)
    new_rows, new_mom_rows = vector_step(row_vectors, sums[6], mom_rows)
    return (block_out, input_grad, sums[0], sums[1], sums[2], sums[3], sums[4], sums[5], sums[6], new_qkv, new_out, new_fc, new_proj, new_bias_qkv, new_bias_fc, new_rows, new_mom_qkv, new_mom_out, new_mom_fc, new_mom_proj, new_mom_bias_qkv, new_mom_bias_fc, new_mom_rows)
```

```python
import math

import jax
import jax.numpy as jnp
from jax import lax
from jax.sharding import PartitionSpec as P

HD = 64
NS_STEPS = 2


eps_norm = 1e-05
eps_gram = 1e-06
coef_a = 3.4445
coef_b = -4.775
coef_c = 2.0315
beta_mom = 0.95
rate_matrix = 0.03
rate_vector = 0.6


def gelu_value(values):
    return jax.nn.gelu(values, approximate=True)


def gelu_slope(values):
    return jax.vjp(gelu_value, values)[1](jnp.ones_like(values))[0]


def product(left_side, right_side, flip_right):
    if flip_right:
        return lax.dot_general(
            left_side, right_side, (((1,), (1,)), ((), ())), preferred_element_type=jnp.float32
        )
    return jnp.dot(left_side, right_side, preferred_element_type=jnp.float32)


def inner_rows(left_side, right_side):
    return lax.dot_general(
        left_side, right_side, (((0,), (0,)), ((), ())), preferred_element_type=jnp.float32
    )


def tile_grid(blocks, first_parts, second_parts):
    height = blocks.shape[1]
    breadth = blocks.shape[2]
    tiled = blocks.reshape(first_parts, second_parts, height, breadth)
    return tiled.transpose(0, 2, 1, 3).reshape(first_parts * height, second_parts * breadth)


def gather_grid(local_piece):
    blocks = lax.all_gather(local_piece, ("col", "row"), axis=0, tiled=False)
    return tile_grid(
        blocks.reshape((-1,) + local_piece.shape), lax.axis_size("col"), lax.axis_size("row")
    )


def norm_stats(values):
    mean_row = jnp.mean(values, axis=1, keepdims=True)
    square = jnp.mean(values * values, axis=1, keepdims=True)
    inv_std = lax.rsqrt(square - mean_row * mean_row + eps_norm)
    return mean_row, inv_std


def matrix_product(left_side, right_side):
    return jnp.dot(
        left_side.astype(jnp.bfloat16),
        right_side.astype(jnp.bfloat16),
        preferred_element_type=jnp.float32,
    )


def polynomial_factor(gram_matrix):
    gram_norm = jnp.sqrt(jnp.sum(gram_matrix * gram_matrix)) + eps_gram
    gram_now = gram_matrix / gram_norm
    poly_before = None
    for repeat in range(NS_STEPS):
        poly = coef_b * gram_now + coef_c * matrix_product(gram_now, gram_now)
        if poly_before is None:
            factor = poly
            scale = coef_a
        else:
            factor = coef_a * factor + scale * poly + matrix_product(poly, factor)
            scale = scale * coef_a
        if repeat + 1 < NS_STEPS:
            half = coef_a * gram_now + matrix_product(poly, gram_now)
            gram_now = coef_a * half + matrix_product(half, poly)
        poly_before = poly
    return factor, scale, gram_norm


def local(
    tokens,
    out_grad,
    segment_ids,
    w_qkv,
    w_out,
    w_fc,
    w_proj,
    bias_qkv,
    bias_fc,
    row_vectors,
    mom_qkv,
    mom_out,
    mom_fc,
    mom_proj,
    mom_bias_qkv,
    mom_bias_fc,
    mom_rows,
):
    low = jnp.bfloat16
    score_scale = 1.0 / math.sqrt(HD)
    row_parts = lax.axis_size("row")
    col_parts = lax.axis_size("col")
    dp_parts = lax.axis_size("dp")
    own_tokens, own_features = tokens.shape
    token_count = own_tokens * col_parts
    feature_count = own_features * row_parts
    token_base = lax.axis_index("col") * own_tokens
    feature_base = lax.axis_index("row") * own_features

    def own_columns(whole):
        return lax.dynamic_slice_in_dim(whole, feature_base, own_features, 1)

    def own_block(whole):
        return lax.dynamic_slice(whole, (token_base, feature_base), (own_tokens, own_features))

    def own_rows(whole):
        return lax.dynamic_slice_in_dim(whole, token_base, own_tokens, 0)

    tokens_all = gather_grid(tokens)
    qkv_cols = lax.all_gather(w_qkv, "row", axis=0, tiled=True)
    vectors_all = lax.all_gather(row_vectors, "row", axis=1, tiled=True)
    out_whole = gather_grid(w_out)
    fc_cols = lax.all_gather(w_fc, "row", axis=0, tiled=True)
    grad_all = gather_grid(out_grad)
    proj_flip = w_proj.T
    proj_cols = lax.all_gather(proj_flip, "row", axis=0, tiled=True)
    gain_one, shift_one, gain_two, shift_two, bias_out, _ = [
        vectors_all[which] for which in range(6)
    ]

    resid_in = tokens_all.astype(jnp.float32)
    mean_one, inv_one = norm_stats(resid_in)
    unit_one = (resid_in - mean_one) * inv_one
    act_one = (unit_one * gain_one + shift_one).astype(low)
    qkv_local = (product(act_one, qkv_cols, False) + bias_qkv).astype(low)
    heads_local = qkv_local.shape[1] // (3 * HD)
    qkv_tiles = qkv_local.reshape(token_count, heads_local, 3, HD).transpose(2, 1, 0, 3)
    query, key, value = qkv_tiles[0], qkv_tiles[1], qkv_tiles[2]
    segment_row = segment_ids[0]
    positions = jnp.arange(token_count, dtype=jnp.int32)
    allowed = (positions[None, :] <= positions[:, None]) & (
        segment_row[None, :] == segment_row[:, None]
    )
    scores = (
        jnp.einsum("hqe,hke->hqk", query, key, preferred_element_type=jnp.float32) * score_scale
    )
    scores = jnp.where(allowed[None], scores, -jnp.inf)
    row_max = jnp.max(scores, axis=2, keepdims=True)
    raised = jnp.exp(scores - row_max)
    probs = raised / jnp.sum(raised, axis=2, keepdims=True)
    prob_low = probs.astype(low)
    attended = jnp.einsum(
        "hqk,hke->hqe", prob_low, value, preferred_element_type=jnp.float32
    ).astype(low)
    attn_local = attended.transpose(1, 0, 2).reshape(token_count, heads_local * HD)
    attn_all = lax.all_gather(attn_local, "col", axis=1, tiled=True)
    resid_mid = resid_in + product(attn_all, out_whole, False) + bias_out
    mean_two, inv_two = norm_stats(resid_mid)
    unit_two = (resid_mid - mean_two) * inv_two
    act_two = (unit_two * gain_two + shift_two).astype(low)
    hidden_pre = product(act_two, fc_cols, False) + bias_fc
    hidden = gelu_value(hidden_pre).astype(low)
    grad_hidden = product(grad_all, proj_cols, False)
    grad_pre = (gelu_slope(hidden_pre) * grad_hidden).astype(low)

    grad_norm_two = lax.psum_scatter(
        product(grad_pre, w_fc, True).astype(low), "col", scatter_dimension=0, tiled=True
    )
    grad_two_all = gather_grid(grad_norm_two).astype(jnp.float32)
    grad_norm_two = grad_norm_two.astype(jnp.float32)
    scaled = grad_two_all * gain_two
    first_mean = jnp.mean(scaled, axis=1, keepdims=True)
    second_mean = jnp.mean(scaled * unit_two, axis=1, keepdims=True)
    grad_mid_all = grad_all.astype(jnp.float32) + inv_two * (
        scaled - first_mean - unit_two * second_mean
    )
    grad_mid_low = grad_mid_all.astype(low)
    out_rows = lax.dynamic_slice_in_dim(
        out_whole, lax.axis_index("col") * w_out.shape[0], w_out.shape[0], 0
    )
    grad_attn = (
        product(grad_mid_low, out_rows, True)
        .astype(low)
        .reshape(token_count, heads_local, HD)
        .transpose(1, 0, 2)
    )

    grad_value = jnp.einsum(
        "hqk,hqe->hke", prob_low, grad_attn, preferred_element_type=jnp.float32
    )
    grad_probs = jnp.einsum("hqe,hke->hqk", grad_attn, value, preferred_element_type=jnp.float32)
    row_dot = jnp.sum(
        grad_attn.astype(jnp.float32) * attended.astype(jnp.float32), axis=2, keepdims=True
    )
    grad_scores = (score_scale * probs * (grad_probs - row_dot)).astype(low)
    grad_query = jnp.einsum("hqk,hke->hqe", grad_scores, key, preferred_element_type=jnp.float32)
    grad_key = jnp.einsum("hqk,hqe->hke", grad_scores, query, preferred_element_type=jnp.float32)
    grad_qkv_low = (
        jnp.stack([grad_query.astype(low), grad_key.astype(low), grad_value.astype(low)], axis=0)
        .transpose(2, 1, 0, 3)
        .reshape(token_count, heads_local * 3 * HD)
    )

    grad_blocks = (
        inner_rows(own_columns(act_one), grad_qkv_low),
        inner_rows(attn_local, own_columns(grad_mid_low)),
        inner_rows(own_columns(act_two), grad_pre),
        inner_rows(hidden, own_columns(grad_all)),
    )
    summed = [lax.psum(block.astype(low), "dp").astype(jnp.float32) for block in grad_blocks]
    bias_sums = lax.psum(
        (
            jnp.sum(grad_qkv_low, axis=0, dtype=jnp.float32),
            jnp.sum(grad_pre, axis=0, dtype=jnp.float32),
        ),
        "dp",
    )
    summed = summed + list(bias_sums)

    weights = (w_qkv, w_out, w_fc, w_proj)
    moments = (mom_qkv, mom_out, mom_fc, mom_proj)
    flips = (False, True, False, True)
    new_moms = [beta_mom * moments[member] + summed[member] for member in range(4)]
    pushes = [
        (summed[member] + beta_mom * new_moms[member]).astype(low) for member in range(4)
    ]
    upright = [pushes[member].T if flips[member] else pushes[member] for member in range(4)]
    widest = max(piece.shape[1] for piece in upright)
    share = -(-widest // dp_parts)
    assert row_parts == len(upright)
    outgoing = jnp.stack(
        [
            jnp.pad(piece, ((0, 0), (0, share * dp_parts - piece.shape[1])))
            for piece in upright
        ]
    )
    outgoing = lax.dynamic_slice_in_dim(outgoing, lax.axis_index("dp") * share, share, 2)
    arrived = lax.all_to_all(outgoing, "row", split_axis=0, concat_axis=0, tiled=True)
    matrix = arrived.reshape(feature_count, share)
    gram = lax.psum(product(matrix, matrix, True).astype(low), ("dp", "col")).astype(jnp.float32)
    factor, scale, gram_norm = polynomial_factor(gram)
    ortho = (scale * matrix.astype(jnp.float32) + matrix_product(factor, matrix)) * lax.rsqrt(
        gram_norm
    )
    back = lax.all_to_all(
        ortho.astype(low).reshape(row_parts, own_features, share),
        "row",
        split_axis=0,
        concat_axis=0,
        tiled=True,
    )
    orthos = lax.all_gather(back, "dp", axis=2, tiled=True)
    new_weights = []
    for member in range(4):
        piece = orthos[member, :, : upright[member].shape[1]]
        if flips[member]:
            piece = piece.T
        longest = max(
            upright[member].shape[0] * row_parts, upright[member].shape[1] * col_parts
        )
        new_weights.append(
            weights[member].astype(jnp.float32)
            - rate_matrix * math.sqrt(longest) * piece.astype(jnp.float32)
        )

    block_sum = lax.psum_scatter(
        product(hidden, proj_flip, True).astype(low), "col", scatter_dimension=0, tiled=True
    ).astype(jnp.float32)
    block_out = (own_block(resid_mid) + block_sum + row_vectors[5]).astype(low)
    grad_norm_one = lax.psum_scatter(
        product(grad_qkv_low, w_qkv, True).astype(low), "col", scatter_dimension=0, tiled=True
    ).astype(jnp.float32)
    unit_one_own = own_block(unit_one)
    scaled_one = grad_norm_one * row_vectors[0]
    first_sum, second_sum = lax.psum(
        (
            jnp.sum(scaled_one, axis=1, keepdims=True),
            jnp.sum(scaled_one * unit_one_own, axis=1, keepdims=True),
        ),
        "row",
    )
    input_grad = own_block(grad_mid_all) + own_rows(inv_one) * (
        scaled_one - first_sum / feature_count - unit_one_own * (second_sum / feature_count)
    )
    row_terms = jnp.stack(
        [
            jnp.sum(grad_norm_one * unit_one_own, axis=0),
            jnp.sum(grad_norm_one, axis=0),
            jnp.sum(grad_norm_two * own_block(unit_two), axis=0),
            jnp.sum(grad_norm_two, axis=0),
            jnp.sum(own_block(grad_mid_low), axis=0, dtype=jnp.float32),
            jnp.sum(out_grad, axis=0, dtype=jnp.float32),
        ]
    )
    grad_rows = lax.psum(row_terms, ("dp", "col"))
    vector_rate = rate_vector / math.sqrt(token_count * dp_parts)

    def vector_step(weight, gradient, moment):
        new_moment = beta_mom * moment + gradient
        return (weight - vector_rate * (gradient + beta_mom * new_moment), new_moment)

    new_bias_qkv, new_mom_bias_qkv = vector_step(bias_qkv, summed[4], mom_bias_qkv)
    new_bias_fc, new_mom_bias_fc = vector_step(bias_fc, summed[5], mom_bias_fc)
    new_rows, new_mom_rows = vector_step(row_vectors, grad_rows, mom_rows)
    return (
        block_out,
        input_grad,
        summed[0],
        summed[1],
        summed[2],
        summed[3],
        summed[4],
        summed[5],
        grad_rows,
        new_weights[0],
        new_weights[1],
        new_weights[2],
        new_weights[3],
        new_bias_qkv,
        new_bias_fc,
        new_rows,
        new_moms[0],
        new_moms[1],
        new_moms[2],
        new_moms[3],
        new_mom_bias_qkv,
        new_mom_bias_fc,
        new_mom_rows,
    )


def solution(mesh):
    placed = (
        P(("dp", "col"), "row"),
        P(("dp", "col"), "row"),
        P("dp", None),
        P("row", "col"),
        P("col", "row"),
        P("row", "col"),
        P("col", "row"),
        P("col"),
        P("col"),
        P(None, "row"),
        P("row", "col"),
        P("col", "row"),
        P("row", "col"),
        P("col", "row"),
        P("col"),
        P("col"),
        P(None, "row"),
    )
    return jax.shard_map(
        local,
        mesh=mesh,
        in_specs=placed,
        out_specs=(
            P(("dp", "col"), "row"),
            P(("dp", "col"), "row"),
            P("row", "col"),
            P("col", "row"),
            P("row", "col"),
            P("col", "row"),
            P("col"),
            P("col"),
            P(None, "row"),
            P("row", "col"),
            P("col", "row"),
            P("row", "col"),
            P("col", "row"),
            P("col"),
            P("col"),
            P(None, "row"),
            P("row", "col"),
            P("col", "row"),
            P("row", "col"),
            P("col", "row"),
            P("col"),
            P("col"),
            P(None, "row"),
        ),
        check_vma=False,
    )
```

```python
import functools
import math

import jax
import jax.numpy as jnp
from jax import lax
from jax.experimental import pallas as pl
from jax.experimental.pallas import tpu as pltpu
from jax.sharding import PartitionSpec as P

HD = 64
NS_STEPS = 2


eps_norm = 1e-05
eps_gram = 1e-06
coef_a = 3.4445
coef_b = -4.775
coef_c = 2.0315
beta_mom = 0.95
rate_matrix = 0.03
rate_vector = 0.6


def gelu_value(values):
    return jax.nn.gelu(values, approximate=True)


def gelu_slope(values):
    return jax.vjp(gelu_value, values)[1](jnp.ones_like(values))[0]


def product(left_side, right_side, flip_right):
    if flip_right:
        return lax.dot_general(
            left_side, right_side, (((1,), (1,)), ((), ())), preferred_element_type=jnp.float32
        )
    return jnp.dot(left_side, right_side, preferred_element_type=jnp.float32)


def inner_rows(left_side, right_side):
    return lax.dot_general(
        left_side, right_side, (((0,), (0,)), ((), ())), preferred_element_type=jnp.float32
    )


def exchange_kernel(axis, parts, kinds, *refs):
    count = len(kinds)
    sources, targets = refs[:count], refs[count : 2 * count]
    send_sem, recv_sem, local_sem = refs[2 * count :]
    me = lax.axis_index(axis)
    barrier = pltpu.get_barrier_semaphore()
    for step in range(1, parts):
        peer = lax.rem(me + step, parts)
        pl.semaphore_signal(
            barrier, inc=1, device_id={axis: peer}, device_id_type=pl.DeviceIdType.MESH
        )
    pl.semaphore_wait(barrier, parts - 1)
    copies = []
    for which in range(count):
        for step in range(1, parts):
            peer = lax.rem(me + step, parts)
            copy = pltpu.make_async_remote_copy(
                src_ref=sources[which].at[peer] if kinds[which] else sources[which],
                dst_ref=targets[which].at[me],
                send_sem=send_sem.at[which, step - 1],
                recv_sem=recv_sem.at[which, step - 1],
                device_id={axis: peer},
                device_id_type=pl.DeviceIdType.MESH,
            )
            copy.start()
            copies.append(copy)
    for which in range(count):
        copy = pltpu.make_async_copy(
            sources[which].at[me] if kinds[which] else sources[which],
            targets[which].at[me],
            local_sem.at[which],
        )
        copy.start()
        copies.append(copy)
    for copy in copies:
        copy.wait()


def exchange(axis, arrays, kinds, name_id):
    parts = lax.axis_size(axis)
    count = len(arrays)
    shapes = [
        jax.ShapeDtypeStruct(
            array.shape if kind else (parts,) + array.shape, array.dtype
        )
        for array, kind in zip(arrays, kinds)
    ]
    return pl.pallas_call(
        functools.partial(exchange_kernel, axis, parts, tuple(kinds)),
        out_shape=shapes,
        in_specs=[pl.BlockSpec(memory_space=pltpu.VMEM)] * count,
        out_specs=[pl.BlockSpec(memory_space=pltpu.VMEM)] * count,
        scratch_shapes=[
            pltpu.SemaphoreType.DMA((count, parts - 1)),
            pltpu.SemaphoreType.DMA((count, parts - 1)),
            pltpu.SemaphoreType.DMA((count,)),
        ],
        compiler_params=pltpu.CompilerParams(collective_id=name_id, has_side_effects=True),
        cost_estimate=pl.CostEstimate(
            flops=0,
            bytes_accessed=sum(shape.size * shape.dtype.itemsize for shape in shapes),
            transcendentals=0,
        ),
    )(*arrays)


def total(slots):
    return jnp.sum(slots.astype(jnp.float32), axis=0)


def gather_grid(local_piece, name_id=None):
    if name_id is None:
        tall = lax.all_gather(local_piece, "col", axis=0, tiled=True)
        return lax.all_gather(tall, "row", axis=1, tiled=True)
    (tall,) = exchange("col", [local_piece], [False], name_id)
    (wide,) = exchange("row", [tall.reshape(-1, tall.shape[2])], [False], name_id + 1)
    return jnp.concatenate([wide[part] for part in range(wide.shape[0])], axis=1)


def norm_stats(values):
    mean_row = jnp.mean(values, axis=1, keepdims=True)
    square = jnp.mean(values * values, axis=1, keepdims=True)
    inv_std = lax.rsqrt(square - mean_row * mean_row + eps_norm)
    return mean_row, inv_std


def matrix_product(left_side, right_side):
    return jnp.dot(
        left_side.astype(jnp.bfloat16),
        right_side.astype(jnp.bfloat16),
        preferred_element_type=jnp.float32,
    )


def polynomial_factor(gram_matrix):
    gram_norm = jnp.sqrt(jnp.sum(gram_matrix * gram_matrix)) + eps_gram
    gram_now = gram_matrix / gram_norm
    poly_before = None
    for repeat in range(NS_STEPS):
        poly = coef_b * gram_now + coef_c * matrix_product(gram_now, gram_now)
        if poly_before is None:
            factor = poly
            scale = coef_a
        else:
            factor = coef_a * factor + scale * poly + matrix_product(poly, factor)
            scale = scale * coef_a
        if repeat + 1 < NS_STEPS:
            half = coef_a * gram_now + matrix_product(poly, gram_now)
            gram_now = coef_a * half + matrix_product(half, poly)
        poly_before = poly
    return factor, scale, gram_norm


def local(
    tokens,
    out_grad,
    segment_ids,
    w_qkv,
    w_out,
    w_fc,
    w_proj,
    bias_qkv,
    bias_fc,
    row_vectors,
    mom_qkv,
    mom_out,
    mom_fc,
    mom_proj,
    mom_bias_qkv,
    mom_bias_fc,
    mom_rows,
):
    low = jnp.bfloat16
    score_scale = 1.0 / math.sqrt(HD)
    row_parts = lax.axis_size("row")
    col_parts = lax.axis_size("col")
    dp_parts = lax.axis_size("dp")
    own_tokens, own_features = tokens.shape
    token_count = own_tokens * col_parts
    feature_count = own_features * row_parts
    token_base = lax.axis_index("col") * own_tokens
    feature_base = lax.axis_index("row") * own_features

    def own_columns(whole):
        return lax.dynamic_slice_in_dim(whole, feature_base, own_features, 1)

    def own_block(whole):
        return lax.dynamic_slice(whole, (token_base, feature_base), (own_tokens, own_features))

    def own_rows(whole):
        return lax.dynamic_slice_in_dim(whole, token_base, own_tokens, 0)

    tokens_all = gather_grid(tokens, 0)
    qkv_cols = lax.all_gather(w_qkv, "row", axis=0, tiled=True)
    (vector_slots,) = exchange("row", [row_vectors], [False], 14)
    vectors_all = jnp.concatenate([vector_slots[part] for part in range(row_parts)], axis=1)
    out_whole = gather_grid(w_out)
    fc_cols = lax.all_gather(w_fc, "row", axis=0, tiled=True)
    grad_all = gather_grid(out_grad)
    proj_flip = w_proj.T
    proj_cols = lax.all_gather(proj_flip, "row", axis=0, tiled=True)
    gain_one, shift_one, gain_two, shift_two, bias_out, _ = [
        vectors_all[which] for which in range(6)
    ]

    resid_in = tokens_all.astype(jnp.float32)
    mean_one, inv_one = norm_stats(resid_in)
    unit_one = (resid_in - mean_one) * inv_one
    act_one = (unit_one * gain_one + shift_one).astype(low)
    qkv_local = (product(act_one, qkv_cols, False) + bias_qkv).astype(low)
    heads_local = qkv_local.shape[1] // (3 * HD)
    qkv_tiles = qkv_local.reshape(token_count, heads_local, 3, HD).transpose(2, 1, 0, 3)
    query, key, value = qkv_tiles[0], qkv_tiles[1], qkv_tiles[2]
    segment_row = segment_ids[0]
    positions = jnp.arange(token_count, dtype=jnp.int32)
    allowed = (positions[None, :] <= positions[:, None]) & (
        segment_row[None, :] == segment_row[:, None]
    )
    scores = (
        jnp.einsum("hqe,hke->hqk", query, key, preferred_element_type=jnp.float32) * score_scale
    )
    scores = jnp.where(allowed[None], scores, -jnp.inf)
    row_max = jnp.max(scores, axis=2, keepdims=True)
    raised = jnp.exp(scores - row_max)
    probs = raised / jnp.sum(raised, axis=2, keepdims=True)
    prob_low = probs.astype(low)
    attended = jnp.einsum(
        "hqk,hke->hqe", prob_low, value, preferred_element_type=jnp.float32
    ).astype(low)
    attn_local = attended.transpose(1, 0, 2).reshape(token_count, heads_local * HD)
    part_tokens = token_count // row_parts
    part_base = lax.axis_index("row") * part_tokens

    def part_rows(whole):
        return lax.dynamic_slice_in_dim(whole, part_base, part_tokens, 0)

    (attn_slots,) = exchange("col", [part_rows(attn_local)], [False], 2)
    attn_part = jnp.concatenate([attn_slots[part] for part in range(col_parts)], axis=1)
    resid_mid = part_rows(resid_in) + product(attn_part, out_whole, False) + bias_out
    mean_two, inv_two = norm_stats(resid_mid)
    unit_two = (resid_mid - mean_two) * inv_two
    act_two = (unit_two * gain_two + shift_two).astype(low)
    hidden_pre = product(act_two, fc_cols, False) + bias_fc
    hidden = gelu_value(hidden_pre).astype(low)
    grad_part = part_rows(grad_all)
    grad_hidden = product(grad_part, proj_cols, False)
    grad_pre = (gelu_slope(hidden_pre) * grad_hidden).astype(low)

    piece_tokens = part_tokens // col_parts
    piece_base = lax.axis_index("col") * piece_tokens

    def piece_rows(part):
        return lax.dynamic_slice_in_dim(part, piece_base, piece_tokens, 0)

    (two_slots,) = exchange(
        "col",
        [product(grad_pre, fc_cols, True).astype(low).reshape(col_parts, piece_tokens, -1)],
        [True],
        3,
    )
    grad_norm_two = total(two_slots)
    unit_two_piece = piece_rows(unit_two)
    scaled = grad_norm_two * gain_two
    first_mean = jnp.mean(scaled, axis=1, keepdims=True)
    second_mean = jnp.mean(scaled * unit_two_piece, axis=1, keepdims=True)
    grad_mid_piece = piece_rows(grad_part).astype(jnp.float32) + piece_rows(inv_two) * (
        scaled - first_mean - unit_two_piece * second_mean
    )
    grad_mid_low = grad_mid_piece.astype(low)
    (mid_slots,) = exchange("col", [grad_mid_low], [False], 4)
    mid_part = mid_slots.reshape(part_tokens, feature_count)
    out_rows = lax.dynamic_slice_in_dim(
        out_whole, lax.axis_index("col") * w_out.shape[0], w_out.shape[0], 0
    )
    grad_attn_part = product(mid_part, out_rows, True).astype(low)
    split = lambda rows: rows.reshape(part_tokens, row_parts, own_features).transpose(1, 0, 2)
    attn_grad_slots, mid_cols, act_two_cols, hidden_slots, grad_pre_slots, resid_cols = exchange(
        "row",
        [
            grad_attn_part,
            split(mid_part),
            split(act_two),
            hidden,
            grad_pre,
            split(resid_mid),
        ],
        [False, True, True, False, False, True],
        5,
    )
    grad_attn = (
        attn_grad_slots.reshape(token_count, heads_local, HD).transpose(1, 0, 2)
    )
    mid_cols = mid_cols.reshape(token_count, own_features)
    act_two_cols = act_two_cols.reshape(token_count, own_features)
    resid_cols = resid_cols.reshape(token_count, own_features)
    hidden_all = hidden_slots.reshape(token_count, -1)
    grad_pre_all = grad_pre_slots.reshape(token_count, -1)

    grad_value = jnp.einsum(
        "hqk,hqe->hke", prob_low, grad_attn, preferred_element_type=jnp.float32
    )
    grad_probs = jnp.einsum("hqe,hke->hqk", grad_attn, value, preferred_element_type=jnp.float32)
    row_dot = jnp.sum(
        grad_attn.astype(jnp.float32) * attended.astype(jnp.float32), axis=2, keepdims=True
    )
    grad_scores = (score_scale * probs * (grad_probs - row_dot)).astype(low)
    grad_query = jnp.einsum("hqk,hke->hqe", grad_scores, key, preferred_element_type=jnp.float32)
    grad_key = jnp.einsum("hqk,hqe->hke", grad_scores, query, preferred_element_type=jnp.float32)
    grad_qkv_low = (
        jnp.stack([grad_query.astype(low), grad_key.astype(low), grad_value.astype(low)], axis=0)
        .transpose(2, 1, 0, 3)
        .reshape(token_count, heads_local * 3 * HD)
    )

    grad_blocks = (
        inner_rows(own_columns(act_one), grad_qkv_low),
        inner_rows(attn_local, mid_cols),
        inner_rows(act_two_cols, grad_pre_all),
        inner_rows(hidden_all, own_columns(grad_all)),
    )
    bias_blocks = jnp.concatenate(
        [
            jnp.sum(grad_qkv_low, axis=0, dtype=jnp.float32),
            jnp.sum(grad_pre_all, axis=0, dtype=jnp.float32),
        ]
    )[None]
    if dp_parts == 2:
        group_slots = exchange(
            "dp", [block.astype(low) for block in grad_blocks] + [bias_blocks], [False] * 5, 6
        )
        summed = [total(slots) for slots in group_slots]
    else:
        summed = [lax.psum(block.astype(low), "dp").astype(jnp.float32) for block in grad_blocks]
        summed.append(lax.psum(bias_blocks, "dp"))
    bias_sums = summed.pop()[0]
    summed = summed + [bias_sums[: bias_qkv.shape[0]], bias_sums[bias_qkv.shape[0] :]]

    weights = (w_qkv, w_out, w_fc, w_proj)
    moments = (mom_qkv, mom_out, mom_fc, mom_proj)
    flips = (False, True, False, True)
    new_moms = [beta_mom * moments[member] + summed[member] for member in range(4)]
    pushes = [
        (summed[member] + beta_mom * new_moms[member]).astype(low) for member in range(4)
    ]
    upright = [pushes[member].T if flips[member] else pushes[member] for member in range(4)]
    widest = max(piece.shape[1] for piece in upright)
    share = -(-widest // dp_parts)
    assert row_parts == len(upright)
    outgoing = jnp.stack(
        [
            jnp.pad(piece, ((0, 0), (0, share * dp_parts - piece.shape[1])))
            for piece in upright
        ]
    )
    outgoing = lax.dynamic_slice_in_dim(outgoing, lax.axis_index("dp") * share, share, 2)
    (arrived,) = exchange("row", [outgoing], [True], 7)
    matrix = arrived.reshape(feature_count, share)
    gram_low = product(matrix, matrix, True).astype(low)
    if dp_parts == 2:
        (half_slots,) = exchange(
            "dp", [gram_low.reshape(dp_parts, -1, feature_count)], [True], 8
        )
        gram_half = total(half_slots).astype(low)
    else:
        gram_half = lax.psum_scatter(gram_low, "dp", scatter_dimension=0, tiled=True)
    if gram_half.shape[0] % (8 * col_parts) == 0:
        (quarter_slots,) = exchange(
            "col", [gram_half.reshape(col_parts, -1, feature_count)], [True], 9
        )
        (whole_slots,) = exchange("col", [total(quarter_slots).astype(low)], [False], 10)
        gram_half = whole_slots.reshape(gram_half.shape)
    else:
        gram_half = lax.psum(gram_half, "col")
    if dp_parts == 2:
        (gram_slots,) = exchange("dp", [gram_half], [False], 11)
        gram = gram_slots.reshape(feature_count, feature_count).astype(jnp.float32)
    else:
        gram = lax.all_gather(gram_half, "dp", axis=0, tiled=True).astype(jnp.float32)
    factor, scale, gram_norm = polynomial_factor(gram)
    ortho = (scale * matrix.astype(jnp.float32) + matrix_product(factor, matrix)) * lax.rsqrt(
        gram_norm
    )
    (back,) = exchange(
        "row", [ortho.astype(low).reshape(row_parts, own_features, share)], [True], 12
    )
    if dp_parts == 2:
        (ortho_slots,) = exchange("dp", [back], [False], 13)
        orthos = jnp.concatenate([ortho_slots[part] for part in range(dp_parts)], axis=2)
    else:
        orthos = lax.all_gather(back, "dp", axis=2, tiled=True)
    new_weights = []
    for member in range(4):
        piece = orthos[member, :, : upright[member].shape[1]]
        if flips[member]:
            piece = piece.T
        longest = max(
            upright[member].shape[0] * row_parts, upright[member].shape[1] * col_parts
        )
        new_weights.append(
            weights[member].astype(jnp.float32)
            - rate_matrix * math.sqrt(longest) * piece.astype(jnp.float32)
        )

    outward = product(hidden_all, proj_flip, True).astype(low)
    inward = product(grad_qkv_low, w_qkv, True).astype(low)
    block_slots, one_slots = exchange(
        "col",
        [
            outward.reshape(col_parts, own_tokens, own_features),
            inward.reshape(col_parts, own_tokens, own_features),
        ],
        [True, True],
        15,
    )
    block_out = (own_rows(resid_cols) + total(block_slots) + row_vectors[5]).astype(low)
    grad_norm_one = total(one_slots)
    unit_one_own = own_block(unit_one)
    scaled_one = grad_norm_one * row_vectors[0]
    stat_pair = jnp.stack(
        [jnp.sum(scaled_one, axis=1), jnp.sum(scaled_one * unit_one_own, axis=1)]
    )
    wide_terms = jnp.stack(
        [
            jnp.sum(grad_norm_two * unit_two_piece, axis=0),
            jnp.sum(grad_norm_two, axis=0),
        ]
    )
    stat_slots, wide_slots = exchange(
        "row",
        [stat_pair, wide_terms.reshape(2, row_parts, own_features).transpose(1, 0, 2)],
        [False, True],
        16,
    )
    stat_sum = total(stat_slots)
    first_sum, second_sum = stat_sum[0][:, None], stat_sum[1][:, None]
    wide_sum = total(wide_slots)
    input_grad = own_rows(mid_cols).astype(jnp.float32) + own_rows(inv_one) * (
        scaled_one - first_sum / feature_count - unit_one_own * (second_sum / feature_count)
    )
    row_terms = jnp.stack(
        [
            jnp.sum(grad_norm_one * unit_one_own, axis=0),
            jnp.sum(grad_norm_one, axis=0),
            wide_sum[0],
            wide_sum[1],
            jnp.sum(own_rows(mid_cols), axis=0, dtype=jnp.float32),
            jnp.sum(out_grad, axis=0, dtype=jnp.float32),
        ]
    )
    (term_slots,) = exchange("col", [row_terms], [False], 17)
    (pair_slots,) = exchange("dp", [total(term_slots)], [False], 18)
    grad_rows = total(pair_slots)
    vector_rate = rate_vector / math.sqrt(token_count * dp_parts)

    def vector_step(weight, gradient, moment):
        new_moment = beta_mom * moment + gradient
        return (weight - vector_rate * (gradient + beta_mom * new_moment), new_moment)

    new_bias_qkv, new_mom_bias_qkv = vector_step(bias_qkv, summed[4], mom_bias_qkv)
    new_bias_fc, new_mom_bias_fc = vector_step(bias_fc, summed[5], mom_bias_fc)
    new_rows, new_mom_rows = vector_step(row_vectors, grad_rows, mom_rows)
    return (
        block_out,
        input_grad,
        summed[0],
        summed[1],
        summed[2],
        summed[3],
        summed[4],
        summed[5],
        grad_rows,
        new_weights[0],
        new_weights[1],
        new_weights[2],
        new_weights[3],
        new_bias_qkv,
        new_bias_fc,
        new_rows,
        new_moms[0],
        new_moms[1],
        new_moms[2],
        new_moms[3],
        new_mom_bias_qkv,
        new_mom_bias_fc,
        new_mom_rows,
    )


def solution(mesh):
    placed = (
        P(("dp", "col"), "row"),
        P(("dp", "col"), "row"),
        P("dp", None),
        P("row", "col"),
        P("col", "row"),
        P("row", "col"),
        P("col", "row"),
        P("col"),
        P("col"),
        P(None, "row"),
        P("row", "col"),
        P("col", "row"),
        P("row", "col"),
        P("col", "row"),
        P("col"),
        P("col"),
        P(None, "row"),
    )
    return jax.shard_map(
        local,
        mesh=mesh,
        in_specs=placed,
        out_specs=(
            P(("dp", "col"), "row"),
            P(("dp", "col"), "row"),
            P("row", "col"),
            P("col", "row"),
            P("row", "col"),
            P("col", "row"),
            P("col"),
            P("col"),
            P(None, "row"),
            P("row", "col"),
            P("col", "row"),
            P("row", "col"),
            P("col", "row"),
            P("col"),
            P("col"),
            P(None, "row"),
            P("row", "col"),
            P("col", "row"),
            P("row", "col"),
            P("col", "row"),
            P("col"),
            P("col"),
            P(None, "row"),
        ),
        check_vma=False,
    )
```

```python
import functools
import math

import jax
import jax.numpy as jnp
from jax import lax
from jax.experimental import pallas as pl
from jax.experimental.pallas import tpu as pltpu
from jax.sharding import PartitionSpec as P

HD = 64
NS_STEPS = 2


eps_norm = 1e-05
eps_gram = 1e-06
coef_a = 3.4445
coef_b = -4.775
coef_c = 2.0315
beta_mom = 0.95
rate_matrix = 0.03
rate_vector = 0.6


def gelu_value(values):
    return jax.nn.gelu(values, approximate=True)


def gelu_slope(values):
    return jax.vjp(gelu_value, values)[1](jnp.ones_like(values))[0]


def product(left_side, right_side, flip_right):
    if flip_right:
        return lax.dot_general(
            left_side, right_side, (((1,), (1,)), ((), ())), preferred_element_type=jnp.float32
        )
    return jnp.dot(left_side, right_side, preferred_element_type=jnp.float32)


def inner_rows(left_side, right_side):
    return lax.dot_general(
        left_side, right_side, (((0,), (0,)), ((), ())), preferred_element_type=jnp.float32
    )


def exchange_kernel(axes, parts, kinds, *refs):
    count = len(kinds)
    sources, targets = refs[:count], refs[count : 2 * count]
    send_sem, recv_sem, local_sem = refs[2 * count :]
    barrier = pltpu.get_barrier_semaphore()
    met = 0
    for axis in sorted(set(axes)):
        axis_parts = parts[axes.index(axis)]
        for step in range(1, axis_parts):
            peer = lax.rem(lax.axis_index(axis) + step, axis_parts)
            pl.semaphore_signal(
                barrier, inc=1, device_id={axis: peer}, device_id_type=pl.DeviceIdType.MESH
            )
            met += 1
    pl.semaphore_wait(barrier, met)
    copies = []
    for which in range(count):
        axis = axes[which]
        me = lax.axis_index(axis)
        for step in range(1, parts[which]):
            peer = lax.rem(me + step, parts[which])
            copy = pltpu.make_async_remote_copy(
                src_ref=sources[which].at[peer] if kinds[which] else sources[which],
                dst_ref=targets[which].at[me],
                send_sem=send_sem.at[which, step - 1],
                recv_sem=recv_sem.at[which, step - 1],
                device_id={axis: peer},
                device_id_type=pl.DeviceIdType.MESH,
            )
            copy.start()
            copies.append(copy)
    for which in range(count):
        me = lax.axis_index(axes[which])
        copy = pltpu.make_async_copy(
            sources[which].at[me] if kinds[which] else sources[which],
            targets[which].at[me],
            local_sem.at[which],
        )
        copy.start()
        copies.append(copy)
    for copy in copies:
        copy.wait()


def exchange(axes, arrays, kinds, name_id):
    count = len(arrays)
    if isinstance(axes, str):
        axes = [axes] * count
    parts = [lax.axis_size(axis) for axis in axes]
    shapes = [
        jax.ShapeDtypeStruct(array.shape if kind else (part,) + array.shape, array.dtype)
        for array, kind, part in zip(arrays, kinds, parts)
    ]
    return pl.pallas_call(
        functools.partial(exchange_kernel, tuple(axes), tuple(parts), tuple(kinds)),
        out_shape=shapes,
        in_specs=[pl.BlockSpec(memory_space=pltpu.VMEM)] * count,
        out_specs=[pl.BlockSpec(memory_space=pltpu.VMEM)] * count,
        scratch_shapes=[
            pltpu.SemaphoreType.DMA((count, max(parts) - 1)),
            pltpu.SemaphoreType.DMA((count, max(parts) - 1)),
            pltpu.SemaphoreType.DMA((count,)),
        ],
        compiler_params=pltpu.CompilerParams(collective_id=name_id, has_side_effects=True),
    )(*arrays)


def total(slots):
    return jnp.sum(slots.astype(jnp.float32), axis=0)


def side_by_side(slots):
    return jnp.concatenate([slots[part] for part in range(slots.shape[0])], axis=1)


def norm_stats(values):
    mean_row = jnp.mean(values, axis=1, keepdims=True)
    square = jnp.mean(values * values, axis=1, keepdims=True)
    inv_std = lax.rsqrt(square - mean_row * mean_row + eps_norm)
    return mean_row, inv_std


def matrix_product(left_side, right_side):
    return jnp.dot(
        left_side.astype(jnp.bfloat16),
        right_side.astype(jnp.bfloat16),
        preferred_element_type=jnp.float32,
    )


def polynomial_factor(gram_matrix):
    gram_norm = jnp.sqrt(jnp.sum(gram_matrix * gram_matrix)) + eps_gram
    gram_now = gram_matrix / gram_norm
    poly_before = None
    for repeat in range(NS_STEPS):
        poly = coef_b * gram_now + coef_c * matrix_product(gram_now, gram_now)
        if poly_before is None:
            factor = poly
            scale = coef_a
        else:
            factor = coef_a * factor + scale * poly + matrix_product(poly, factor)
            scale = scale * coef_a
        if repeat + 1 < NS_STEPS:
            half = coef_a * gram_now + matrix_product(poly, gram_now)
            gram_now = coef_a * half + matrix_product(half, poly)
        poly_before = poly
    return factor, scale, gram_norm


def local(
    tokens,
    out_grad,
    segment_ids,
    w_qkv,
    w_out,
    w_fc,
    w_proj,
    bias_qkv,
    bias_fc,
    row_vectors,
    mom_qkv,
    mom_out,
    mom_fc,
    mom_proj,
    mom_bias_qkv,
    mom_bias_fc,
    mom_rows,
):
    low = jnp.bfloat16
    score_scale = 1.0 / math.sqrt(HD)
    row_parts = lax.axis_size("row")
    col_parts = lax.axis_size("col")
    dp_parts = lax.axis_size("dp")
    own_tokens, own_features = tokens.shape
    token_count = own_tokens * col_parts
    feature_count = own_features * row_parts
    token_base = lax.axis_index("col") * own_tokens
    feature_base = lax.axis_index("row") * own_features

    def own_columns(whole):
        return lax.dynamic_slice_in_dim(whole, feature_base, own_features, 1)

    def own_block(whole):
        return lax.dynamic_slice(whole, (token_base, feature_base), (own_tokens, own_features))

    def own_rows(whole):
        return lax.dynamic_slice_in_dim(whole, token_base, own_tokens, 0)

    proj_flip = w_proj.T
    tokens_tall, grad_tall, out_tall = exchange(
        "col", [tokens, out_grad, w_out.T], [False] * 3, 0
    )
    grad_cols = grad_tall.reshape(token_count, own_features)
    matrices = [w_qkv, side_by_side(out_tall), w_fc, proj_flip]
    halved = dp_parts == 2
    pieces = matrices
    if halved:
        piece_size = own_features // 2
        pieces = [
            lax.dynamic_slice_in_dim(whole, lax.axis_index("dp") * piece_size, piece_size, 0)
            for whole in matrices
        ]
    token_slots, grad_slots, vector_slots, *gathered = exchange(
        "row",
        [
            tokens_tall.reshape(token_count, own_features),
            grad_cols.reshape(row_parts, -1, own_features),
            row_vectors,
        ]
        + pieces,
        [False, True, False] + [False] * 4,
        1,
    )
    if halved:
        gathered = [
            both.transpose(1, 0, 2, 3)
            for both in exchange("dp", gathered, [False] * 4, 19)
        ]
    qkv_cols, out_flip, fc_cols, proj_cols = [
        slots.reshape(feature_count, -1) for slots in gathered
    ]
    tokens_all = side_by_side(token_slots)
    grad_part = side_by_side(grad_slots)
    vectors_all = side_by_side(vector_slots)
    gain_one, shift_one, gain_two, shift_two, bias_out, _ = [
        vectors_all[which] for which in range(6)
    ]

    resid_in = tokens_all.astype(jnp.float32)
    mean_one, inv_one = norm_stats(resid_in)
    unit_one = (resid_in - mean_one) * inv_one
    act_one = (unit_one * gain_one + shift_one).astype(low)
    qkv_local = (product(act_one, qkv_cols, False) + bias_qkv).astype(low)
    heads_local = qkv_local.shape[1] // (3 * HD)
    qkv_tiles = qkv_local.reshape(token_count, heads_local, 3, HD).transpose(2, 1, 0, 3)
    query, key, value = qkv_tiles[0], qkv_tiles[1], qkv_tiles[2]
    segment_row = segment_ids[0]
    positions = jnp.arange(token_count, dtype=jnp.int32)
    allowed = (positions[None, :] <= positions[:, None]) & (
        segment_row[None, :] == segment_row[:, None]
    )
    scores = (
        jnp.einsum("hqe,hke->hqk", query, key, preferred_element_type=jnp.float32) * score_scale
    )
    scores = jnp.where(allowed[None], scores, -jnp.inf)
    row_max = jnp.max(scores, axis=2, keepdims=True)
    raised = jnp.exp(scores - row_max)
    probs = raised / jnp.sum(raised, axis=2, keepdims=True)
    prob_low = probs.astype(low)
    attended = jnp.einsum(
        "hqk,hke->hqe", prob_low, value, preferred_element_type=jnp.float32
    ).astype(low)
    attn_local = attended.transpose(1, 0, 2).reshape(token_count, heads_local * HD)
    part_tokens = token_count // row_parts
    part_base = lax.axis_index("row") * part_tokens

    def part_rows(whole):
        return lax.dynamic_slice_in_dim(whole, part_base, part_tokens, 0)

    (attn_slots,) = exchange("col", [part_rows(attn_local)], [False], 2)
    attn_part = jnp.concatenate([attn_slots[part] for part in range(col_parts)], axis=1)
    resid_mid = part_rows(resid_in) + product(attn_part, out_flip, True) + bias_out
    mean_two, inv_two = norm_stats(resid_mid)
    unit_two = (resid_mid - mean_two) * inv_two
    act_two = (unit_two * gain_two + shift_two).astype(low)
    hidden_pre = product(act_two, fc_cols, False) + bias_fc
    hidden = gelu_value(hidden_pre).astype(low)
    grad_hidden = product(grad_part, proj_cols, False)
    grad_pre = (gelu_slope(hidden_pre) * grad_hidden).astype(low)

    piece_tokens = part_tokens // col_parts
    piece_base = lax.axis_index("col") * piece_tokens

    def piece_rows(part):
        return lax.dynamic_slice_in_dim(part, piece_base, piece_tokens, 0)

    (two_slots,) = exchange(
        "col",
        [product(grad_pre, fc_cols, True).astype(low).reshape(col_parts, piece_tokens, -1)],
        [True],
        3,
    )
    grad_norm_two = total(two_slots)
    unit_two_piece = piece_rows(unit_two)
    scaled = grad_norm_two * gain_two
    first_mean = jnp.mean(scaled, axis=1, keepdims=True)
    second_mean = jnp.mean(scaled * unit_two_piece, axis=1, keepdims=True)
    grad_mid_piece = piece_rows(grad_part).astype(jnp.float32) + piece_rows(inv_two) * (
        scaled - first_mean - unit_two_piece * second_mean
    )
    grad_mid_low = grad_mid_piece.astype(low)
    (mid_slots,) = exchange("col", [grad_mid_low], [False], 4)
    mid_part = mid_slots.reshape(part_tokens, feature_count)
    out_rows = lax.dynamic_slice_in_dim(
        out_flip, lax.axis_index("col") * w_out.shape[0], w_out.shape[0], 1
    )
    grad_attn_part = product(mid_part, out_rows, False).astype(low)
    split = lambda rows: rows.reshape(part_tokens, row_parts, own_features).transpose(1, 0, 2)
    attn_grad_slots, mid_cols, act_two_cols, hidden_slots, grad_pre_slots, resid_cols = exchange(
        "row",
        [
            grad_attn_part,
            split(mid_part),
            split(act_two),
            hidden,
            grad_pre,
            split(resid_mid),
        ],
        [False, True, True, False, False, True],
        5,
    )
    grad_attn = (
        attn_grad_slots.reshape(token_count, heads_local, HD).transpose(1, 0, 2)
    )
    mid_cols = mid_cols.reshape(token_count, own_features)
    act_two_cols = act_two_cols.reshape(token_count, own_features)
    resid_cols = resid_cols.reshape(token_count, own_features)
    hidden_all = hidden_slots.reshape(token_count, -1)
    grad_pre_all = grad_pre_slots.reshape(token_count, -1)

    grad_value = jnp.einsum(
        "hqk,hqe->hke", prob_low, grad_attn, preferred_element_type=jnp.float32
    )
    grad_probs = jnp.einsum("hqe,hke->hqk", grad_attn, value, preferred_element_type=jnp.float32)
    row_dot = jnp.sum(
        grad_attn.astype(jnp.float32) * attended.astype(jnp.float32), axis=2, keepdims=True
    )
    grad_scores = (score_scale * probs * (grad_probs - row_dot)).astype(low)
    grad_query = jnp.einsum("hqk,hke->hqe", grad_scores, key, preferred_element_type=jnp.float32)
    grad_key = jnp.einsum("hqk,hqe->hke", grad_scores, query, preferred_element_type=jnp.float32)
    grad_qkv_low = (
        jnp.stack([grad_query.astype(low), grad_key.astype(low), grad_value.astype(low)], axis=0)
        .transpose(2, 1, 0, 3)
        .reshape(token_count, heads_local * 3 * HD)
    )

    grad_blocks = (
        inner_rows(own_columns(act_one), grad_qkv_low),
        inner_rows(attn_local, mid_cols),
        inner_rows(act_two_cols, grad_pre_all),
        inner_rows(hidden_all, grad_cols),
    )
    bias_blocks = jnp.concatenate(
        [
            jnp.sum(grad_qkv_low, axis=0, dtype=jnp.float32),
            jnp.sum(grad_pre_all, axis=0, dtype=jnp.float32),
        ]
    )[None]
    if dp_parts == 2:
        group_slots = exchange(
            "dp", [block.astype(low) for block in grad_blocks] + [bias_blocks], [False] * 5, 6
        )
        summed = [total(slots) for slots in group_slots]
    else:
        summed = [lax.psum(block.astype(low), "dp").astype(jnp.float32) for block in grad_blocks]
        summed.append(lax.psum(bias_blocks, "dp"))
    bias_sums = summed.pop()[0]
    summed = summed + [bias_sums[: bias_qkv.shape[0]], bias_sums[bias_qkv.shape[0] :]]

    weights = (w_qkv, w_out, w_fc, w_proj)
    moments = (mom_qkv, mom_out, mom_fc, mom_proj)
    flips = (False, True, False, True)
    new_moms = [beta_mom * moments[member] + summed[member] for member in range(4)]
    pushes = [
        (summed[member] + beta_mom * new_moms[member]).astype(low) for member in range(4)
    ]
    upright = [pushes[member].T if flips[member] else pushes[member] for member in range(4)]
    widest = max(piece.shape[1] for piece in upright)
    share = -(-widest // dp_parts)
    assert row_parts == len(upright)
    outgoing = jnp.stack(
        [
            jnp.pad(piece, ((0, 0), (0, share * dp_parts - piece.shape[1])))
            for piece in upright
        ]
    )
    outgoing = lax.dynamic_slice_in_dim(outgoing, lax.axis_index("dp") * share, share, 2)
    outward = product(hidden_all, proj_flip, True).astype(low)
    inward = product(grad_qkv_low, w_qkv, True).astype(low)
    arrived, block_slots, one_slots = exchange(
        ["row", "col", "col"],
        [
            outgoing,
            outward.reshape(col_parts, own_tokens, own_features),
            inward.reshape(col_parts, own_tokens, own_features),
        ],
        [True] * 3,
        7,
    )
    matrix = arrived.reshape(feature_count, share)
    gram_low = product(matrix, matrix, True).astype(low)
    edge = feature_count // 3
    spots = [(0, 0), (0, 1), (0, 2), (1, 1), (1, 2), (2, 2)]
    packed = jnp.concatenate(
        [
            gram_low[up * edge : (up + 1) * edge, across * edge : (across + 1) * edge]
            for up, across in spots
        ],
        axis=0,
    )
    block_out = (own_rows(resid_cols) + total(block_slots) + row_vectors[5]).astype(low)
    grad_norm_one = total(one_slots)
    unit_one_own = own_block(unit_one)
    scaled_one = grad_norm_one * row_vectors[0]
    stat_pair = jnp.stack(
        [jnp.sum(scaled_one, axis=1), jnp.sum(scaled_one * unit_one_own, axis=1)]
    )
    wide_terms = jnp.stack(
        [
            jnp.sum(grad_norm_two * unit_two_piece, axis=0),
            jnp.sum(grad_norm_two, axis=0),
        ]
    )
    wide_slot_terms = wide_terms.reshape(2, row_parts, own_features).transpose(1, 0, 2)
    if dp_parts == 2:
        stat_slots, wide_slots, half_slots = exchange(
            ["row", "row", "dp"],
            [stat_pair, wide_slot_terms, packed.reshape(dp_parts, -1, edge)],
            [False, True, True],
            8,
        )
        gram_half = total(half_slots).astype(low)
    else:
        stat_slots, wide_slots = exchange(
            "row", [stat_pair, wide_slot_terms], [False, True], 8
        )
        gram_half = lax.psum(packed, "dp")
    stat_sum = total(stat_slots)
    first_sum, second_sum = stat_sum[0][:, None], stat_sum[1][:, None]
    wide_sum = total(wide_slots)
    input_grad = own_rows(mid_cols).astype(jnp.float32) + own_rows(inv_one) * (
        scaled_one - first_sum / feature_count - unit_one_own * (second_sum / feature_count)
    )
    row_terms = jnp.stack(
        [
            jnp.sum(grad_norm_one * unit_one_own, axis=0),
            jnp.sum(grad_norm_one, axis=0),
            wide_sum[0],
            wide_sum[1],
            jnp.sum(own_rows(mid_cols), axis=0, dtype=jnp.float32),
            jnp.sum(out_grad, axis=0, dtype=jnp.float32),
        ]
    )
    quarter_slots, term_slots = exchange(
        "col",
        [gram_half.reshape(col_parts, -1, edge), row_terms],
        [True, False],
        9,
    )
    (whole_slots,) = exchange("col", [total(quarter_slots).astype(low)], [False], 10)
    gram_half = whole_slots.reshape(gram_half.shape)
    if dp_parts == 2:
        gram_slots, pair_slots = exchange(
            "dp", [gram_half, total(term_slots)], [False, False], 11
        )
        gram_half = gram_slots
    else:
        (pair_slots,) = exchange("dp", [total(term_slots)], [False], 11)
    grad_rows = total(pair_slots)
    tiles = gram_half.reshape(len(spots), edge, edge)
    found = {spot: tiles[which] for which, spot in enumerate(spots)}
    gram = jnp.concatenate(
        [
            jnp.concatenate(
                [
                    found[up, across] if across >= up else found[across, up].T
                    for across in range(3)
                ],
                axis=1,
            )
            for up in range(3)
        ],
        axis=0,
    ).astype(jnp.float32)
    factor, scale, gram_norm = polynomial_factor(gram)
    ortho = (scale * matrix.astype(jnp.float32) + matrix_product(factor, matrix)) * lax.rsqrt(
        gram_norm
    )
    (back,) = exchange(
        "row", [ortho.astype(low).reshape(row_parts, own_features, share)], [True], 12
    )
    if dp_parts == 2:
        (ortho_slots,) = exchange("dp", [back], [False], 13)
        orthos = jnp.concatenate([ortho_slots[part] for part in range(dp_parts)], axis=2)
    else:
        orthos = lax.all_gather(back, "dp", axis=2, tiled=True)
    new_weights = []
    for member in range(4):
        piece = orthos[member, :, : upright[member].shape[1]]
        if flips[member]:
            piece = piece.T
        longest = max(
            upright[member].shape[0] * row_parts, upright[member].shape[1] * col_parts
        )
        new_weights.append(
            weights[member].astype(jnp.float32)
            - rate_matrix * math.sqrt(longest) * piece.astype(jnp.float32)
        )

    vector_rate = rate_vector / math.sqrt(token_count * dp_parts)

    def vector_step(weight, gradient, moment):
        new_moment = beta_mom * moment + gradient
        return (weight - vector_rate * (gradient + beta_mom * new_moment), new_moment)

    new_bias_qkv, new_mom_bias_qkv = vector_step(bias_qkv, summed[4], mom_bias_qkv)
    new_bias_fc, new_mom_bias_fc = vector_step(bias_fc, summed[5], mom_bias_fc)
    new_rows, new_mom_rows = vector_step(row_vectors, grad_rows, mom_rows)
    return (
        block_out,
        input_grad,
        summed[0],
        summed[1],
        summed[2],
        summed[3],
        summed[4],
        summed[5],
        grad_rows,
        new_weights[0],
        new_weights[1],
        new_weights[2],
        new_weights[3],
        new_bias_qkv,
        new_bias_fc,
        new_rows,
        new_moms[0],
        new_moms[1],
        new_moms[2],
        new_moms[3],
        new_mom_bias_qkv,
        new_mom_bias_fc,
        new_mom_rows,
    )


def solution(mesh):
    placed = (
        P(("dp", "col"), "row"),
        P(("dp", "col"), "row"),
        P("dp", None),
        P("row", "col"),
        P("col", "row"),
        P("row", "col"),
        P("col", "row"),
        P("col"),
        P("col"),
        P(None, "row"),
        P("row", "col"),
        P("col", "row"),
        P("row", "col"),
        P("col", "row"),
        P("col"),
        P("col"),
        P(None, "row"),
    )
    return jax.shard_map(
        local,
        mesh=mesh,
        in_specs=placed,
        out_specs=(
            P(("dp", "col"), "row"),
            P(("dp", "col"), "row"),
            P("row", "col"),
            P("col", "row"),
            P("row", "col"),
            P("col", "row"),
            P("col"),
            P("col"),
            P(None, "row"),
            P("row", "col"),
            P("col", "row"),
            P("row", "col"),
            P("col", "row"),
            P("col"),
            P("col"),
            P(None, "row"),
            P("row", "col"),
            P("col", "row"),
            P("row", "col"),
            P("col", "row"),
            P("col"),
            P("col"),
            P(None, "row"),
        ),
        check_vma=False,
    )
```
